512 devices in a mesh: var: 16 (over x, y_hi, core), tm: 32 (over z, y_lo).
Axes of the slice: x: 4, y: 8 (y_hi: 2, y_lo: 4; y = y_hi * 4 + y_lo), z: 8, core: 2. Of those that a mesh axis runs over, the one named last changes fastest.
Arguments:
- latent: bfloat16 [16, 8192, 1536], P('var', 'tm')
- fresh_noise: bfloat16 [16, 8192, 1536], P('var', 'tm'), may hold values from -6 to 6
- timestep: int32 [1], replicated, may hold values from 400 to 800
- prompt_ids: int32 [16, 64], P('var'), may hold values from 0 to 16383
- block_table: int32 [3, 3], replicated, may hold values from 0 to 1, as said below
- prompt_table: bfloat16 [16384, 1536], P(None, 'tm'), may hold values from -12 to 12
- w_query: bfloat16 [1536, 768], P('var')
- w_keyval: bfloat16 [1536, 1536], P('var')
- w_out: bfloat16 [768, 1536], P('var'), may hold values from -0.4375 to 0.4375
Outputs:
- stepped: bfloat16 [16, 8192, 1536], P('var', 'tm')
The draws below stay inside these ranges and needn't reach their ends.
Inputs may be any that keep to these rules, and one draw needn't show every extreme that they name: `block_table`: the diagonal and the first column of the table are always 1.
All inputs are finite; a program needn't handle non-finite values.
Results may differ from the reference program's by a relative error of at most 0.0048.
Values may be sent and summed in bfloat16 or wider, within the bound.
A program may use at most 64 MiB of HBM per device.

```python
import math
import jax
import jax.numpy as jnp
from jax import lax

D = 1536
HEADS = 12
HS = 64
HD = 768
VOCAB = 16384
PROMPT = 64
CH = 256
SEAM = 128
BLK = 128
NBLK = 3
TSTEPS = 1000
STRIDE = 200
VARS = 16
FRAMES = 8192
N_TM = 32


def draw_latent(key, part):
    base_key, row_key, column_key = jax.random.split(key, 3)
    base = jax.random.normal(base_key, (VARS, FRAMES, D), jnp.float32)
    row_scale = jnp.exp(jax.random.uniform(row_key, (VARS, FRAMES, 1), jnp.float32, math.log(0.3), math.log(3.0)))
    column_scale = jnp.exp(jax.random.uniform(column_key, (D,), jnp.float32, math.log(0.3), math.log(3.0)))
    return (base * row_scale * column_scale).astype(jnp.bfloat16)


def draw_block_table(key, part):
    picks = jax.random.randint(key, (NBLK, NBLK), 0, 2)
    positions = jnp.arange(NBLK)
    forced = (positions[:, None] == positions[None, :]) | (positions[None, :] == 0)
    return jnp.where(forced, 1, picks).astype(jnp.int32)


def projection_parts(key):
    query_part = jax.random.normal(jax.random.fold_in(key, 11), (D, HD), jnp.float32) / math.sqrt(D)
    key_part = jax.random.normal(jax.random.fold_in(key, 12), (D, HD), jnp.float32) / math.sqrt(D)
    value_part = jax.random.normal(jax.random.fold_in(key, 13), (D, HD), jnp.float32) / math.sqrt(D)
    return (query_part, key_part, value_part)


def draw_w_query(key, part):
    query_part, key_part, value_part = projection_parts(key)
    return query_part.astype(jnp.bfloat16)


def draw_w_keyval(key, part):
    query_part, key_part, value_part = projection_parts(key)
    return jnp.concatenate([key_part, value_part], axis=1).astype(jnp.bfloat16)


def with_ends(entries, stream_key, smallest, high):
    spot = [jax.random.randint(jax.random.fold_in(stream_key, axis), (), 0, length) for axis, length in enumerate(entries.shape)]
    longest = entries.shape.index(max(entries.shape))
    beside = spot[:longest] + [(spot[longest] + 1) % entries.shape[longest]] + spot[longest + 1:]
    return entries.at[tuple(spot)].set(smallest).at[tuple(beside)].set(high)


def level_of(own_key, dims, cuts, smallest, largest):
    loudness, own = 1.0, jax.random.fold_in(own_key, 6)
    for axis_at, parts in cuts:
        heights = jnp.exp(jax.random.uniform(jax.random.fold_in(own, axis_at), (parts,), jnp.float32, smallest / len(cuts), largest / len(cuts)))
        loudness = loudness * jnp.repeat(heights, dims[axis_at] // parts).reshape([-1 if axis == axis_at else 1 for axis in range(len(dims))])
    return loudness


def centred(stream_key, shape, scale, bound, cuts=(), kind=jnp.bfloat16):
    factor_of = level_of(stream_key, shape, cuts, -0.22, 0.18) if cuts else 1.0
    drawn = jax.random.normal(stream_key, shape, jnp.float32) * scale * factor_of
    return jnp.minimum(jnp.maximum(drawn, -bound), bound).astype(kind)


def setup_inputs(seed: int = 0) -> dict:
    arg_keys = jax.random.split(jax.random.key(seed), 10)
    latent = draw_latent(jax.random.fold_in(arg_keys[9], 71), 0)
    fresh_noise = centred(arg_keys[1], (VARS, FRAMES, D), 1.0, 6.0, ((0, 16), (1, 32)))
    timestep = jax.random.randint(arg_keys[2], (1,), 400, 801).astype(jnp.int32)
    prompt_ids = with_ends(jax.random.randint(arg_keys[3], (VARS, PROMPT), 0, VOCAB), jax.random.fold_in(arg_keys[3], 1), 0, VOCAB - 1).astype(jnp.int32)
    block_table = draw_block_table(jax.random.fold_in(arg_keys[9], 71), 0)
    prompt_table = centred(arg_keys[5], (VOCAB, D), 2.0, 12.0, ((1, 32),))
    w_query = draw_w_query(jax.random.fold_in(arg_keys[9], 71), 0)
    w_keyval = draw_w_keyval(jax.random.fold_in(arg_keys[9], 71), 0)
    w_out = centred(arg_keys[8], (HD, D), 0.07, 0.4375, ((0, 16),))
    return {"latent": latent, "fresh_noise": fresh_noise, "timestep": timestep, "prompt_ids": prompt_ids, "block_table": block_table, "prompt_table": prompt_table, "w_query": w_query, "w_keyval": w_keyval, "w_out": w_out}


epsilon = 1e-06

def plan(moment):
    return jnp.cos((moment / TSTEPS + 0.008) / 1.008 * (math.pi / 2.0)) ** 2

def coefficients(timestep):
    current = timestep[0].astype(jnp.float32)
    abar_now = plan(current)
    abar_prev = plan(current - STRIDE)
    spread = jnp.sqrt((1.0 - abar_prev) / (1.0 - abar_now) * (1.0 - abar_now / abar_prev))
    carried = jnp.sqrt((1.0 - abar_prev) * (abar_now / abar_prev - abar_now) / (1.0 - abar_now))
    coef_pred = carried - jnp.sqrt(abar_prev) * jnp.sqrt(1.0 - abar_now) / jnp.sqrt(abar_now)
    coef_latent = jnp.sqrt(abar_prev / abar_now)
    return (current, coef_latent, coef_pred, spread)

def time_embedding(current, model_width):
    half_width = model_width // 2
    frequency = jnp.exp(-math.log(10000.0) * jnp.arange(half_width, dtype=jnp.float32) / half_width)
    angles = current * frequency
    return jnp.concatenate([jnp.cos(angles), jnp.sin(angles)])

def reference(latent, fresh_noise, timestep, prompt_ids, block_table, prompt_table, w_query, w_keyval, w_out):
    current, coef_latent, coef_pred, spread = coefficients(timestep)
    embedded = time_embedding(current, D)
    pooled = lax.optimization_barrier(jnp.mean(prompt_table[prompt_ids].astype(jnp.float32), axis=1))
    condition = embedded[None, :] + pooled

    def normalize_project(operands):
        latent_rows, condition_row = operands
        values = latent_rows.astype(jnp.float32)
        inv_norm = lax.rsqrt(lax.optimization_barrier(jnp.mean(values * values, axis=-1, keepdims=True)) + epsilon)
        normed = (values * inv_norm * (1.0 + condition_row[None, :])).astype(jnp.bfloat16)
        queries = jnp.dot(normed, w_query, preferred_element_type=jnp.float32).astype(jnp.bfloat16)
        keyvals = jnp.dot(normed, w_keyval, preferred_element_type=jnp.float32).astype(jnp.bfloat16)
        return (queries, keyvals)
    queries, keyvals = lax.map(normalize_project, (latent, condition))
    queries = jnp.pad(queries, ((0, 0), (0, SEAM), (0, 0)))
    keyvals = jnp.pad(keyvals, ((0, 0), (0, SEAM), (0, 0)))
    window_rows = CH + SEAM
    allowed = jnp.repeat(jnp.repeat(block_table, BLK, axis=0), BLK, axis=1) > 0

    def one_window(flat_index):
        variant = flat_index // N_TM
        segment = flat_index % N_TM
        offset = (segment * CH).astype(jnp.int32)
        own_query = lax.dynamic_slice_in_dim(queries[variant], offset, window_rows, 0)
        own_keyval = lax.dynamic_slice_in_dim(keyvals[variant], offset, window_rows, 0)
        source_keyval = lax.dynamic_slice_in_dim(keyvals[0], offset, window_rows, 0)
        key_valid = offset + jnp.arange(window_rows, dtype=jnp.int32) < FRAMES
        key_mask = allowed & key_valid[None, :]
        both_masks = jnp.concatenate([key_mask, key_mask], axis=1)
        all_keys = jnp.concatenate([own_keyval[:, :HD], source_keyval[:, :HD]], axis=0)
        all_values = jnp.concatenate([own_keyval[:, HD:], source_keyval[:, HD:]], axis=0)
        query_heads = own_query.astype(jnp.float32).reshape(window_rows, HEADS, HS)
        key_heads = all_keys.astype(jnp.float32).reshape(2 * window_rows, HEADS, HS)
        value_heads = all_values.astype(jnp.float32).reshape(2 * window_rows, HEADS, HS)
        scores = jnp.einsum('qhd,khd->hqk', query_heads, key_heads) * (1.0 / math.sqrt(HS))
        scores = jnp.where(both_masks[None], scores, -1e+30)
        row_max = lax.optimization_barrier(jnp.max(scores, axis=-1, keepdims=True))
        weights = jnp.exp(scores - row_max)
        row_sum = lax.optimization_barrier(jnp.sum(weights, axis=-1, keepdims=True))
        probs = (weights / row_sum).astype(jnp.bfloat16)
        attended = jnp.einsum('hqk,khd->qhd', probs.astype(jnp.float32), value_heads)
        return attended.reshape(window_rows, HD)
    windows = lax.map(one_window, jnp.arange(VARS * N_TM, dtype=jnp.int32))
    windows = windows.reshape(VARS, N_TM, window_rows, HD)
    ramp_up = (jnp.arange(SEAM, dtype=jnp.float32) + 0.5) / SEAM
    tails = windows[:, :, CH:, :] * (1.0 - ramp_up)[None, None, :, None]
    carried = jnp.concatenate([jnp.zeros_like(tails[:, :1]), tails[:, :-1]], axis=1)
    lead_weight = jnp.where((jnp.arange(N_TM) == 0)[:, None], 1.0, ramp_up[None, :])
    lead_part = windows[:, :, :SEAM, :] * lead_weight[None, :, :, None] + carried
    blended = jnp.concatenate([lead_part, windows[:, :, SEAM:CH, :]], axis=2)
    blended = blended.astype(jnp.bfloat16).reshape(VARS, FRAMES, HD)

    def finish(operands):
        blended_rows, latent_rows, noise_rows = operands
        prediction = jnp.dot(blended_rows, w_out, preferred_element_type=jnp.float32)
        result = coef_latent * latent_rows.astype(jnp.float32) + coef_pred * prediction + spread * noise_rows.astype(jnp.float32)
        return result.astype(jnp.bfloat16)
    return lax.map(finish, (blended, latent, fresh_noise))
```

```python
import math

import jax
import jax.numpy as jnp
from jax import lax
from jax.experimental import pallas as pl
from jax.experimental.pallas import tpu as pltpu
from jax.sharding import PartitionSpec as P

MESH = pl.DeviceIdType.MESH
F32 = jnp.float32
BF16 = jnp.bfloat16

D = 1536
HD = 768
CH = 256
SEAM = 128
WIN = CH + SEAM
PROMPT = 64
TSTEPS = 1000
STRIDE = 200
NX, NZ, NL = 4, 8, 4
EPS = 1e-06
QP, KP, VP, OP = 0, 1, 2, 3


def plan(moment):
    return jnp.cos((moment / TSTEPS + 0.008) / 1.008 * (math.pi / 2.0)) ** 2


def coefficients(timestep):
    current = timestep[0].astype(F32)
    abar_now = plan(current)
    abar_prev = plan(current - STRIDE)
    spread = jnp.sqrt((1.0 - abar_prev) / (1.0 - abar_now) * (1.0 - abar_now / abar_prev))
    carried = jnp.sqrt((1.0 - abar_prev) * (abar_now / abar_prev - abar_now) / (1.0 - abar_now))
    coef_pred = carried - jnp.sqrt(abar_prev) * jnp.sqrt(1.0 - abar_now) / jnp.sqrt(abar_now)
    coef_latent = jnp.sqrt(abar_prev / abar_now)
    return (current, coef_latent, coef_pred, spread)


def time_embedding(current):
    half_width = D // 2
    frequency = jnp.exp(-math.log(10000.0) * jnp.arange(half_width, dtype=F32) / half_width)
    angles = current * frequency
    return jnp.concatenate([jnp.cos(angles), jnp.sin(angles)])


def window_tile(tm):
    return min(48 * tm // 128, 10)


def kernel(
    latent, noise, embedded, coefs, block_table, prompt_ids, table, w_query, w_keyval, w_out,
    out,
    wqkv, wo, xw, sp, xn, tabv, counts, mine, pooled, q_s, k_s, v_s, s_s, p_s, blended, tail_out, tail_in, noise_v,
    loc, xs, xr, x2s, x2r, ys, yr, zs, zr, ss, sr,
    s0s, s0r, s1s, s1r, s2s, s2r, s3s, s3r, s4s, s4r, seam_s, seam_r, tail_s, tail_r,
    p0s, p0r, p1s, p1r, p2s, p2r,
):
    var, tm = lax.axis_index("var"), lax.axis_index("tm")
    x, yh, c = var // 4, (var // 2) % 2, var % 2
    z, yl = tm // NL, tm % NL
    par = z % 2
    y = yh * NL + yl
    xm, xp, xq = (x + 3) % NX, (x + 1) % NX, (x + 2) % NX
    y_up, y_dn = (y + 1) % 8, (y + 7) % 8

    def at(x_, yh_, c_, z_, yl_):
        return {"var": (x_ * 2 + yh_) * 2 + c_, "tm": z_ * NL + yl_}

    sib = at(x, yh, 1 - c, z, yl)
    x_left, x_right = at(xm, yh, c, z, yl), at(xp, yh, c, z, yl)
    y_next = at(x, y_up // NL, c, z, y_up % NL)
    y_prev = at(x, y_dn // NL, c, z, y_dn % NL)
    z_next, z_prev = at(x, yh, c, (z + 1) % NZ, yl), at(x, yh, c, (z + 7) % NZ, yl)
    partner = at(x, 1 - yh, c, z, yl)
    tm_next, tm_prev = {"var": var, "tm": (tm + 1) % 32}, {"var": var, "tm": (tm + 31) % 32}
    src_here, src_next = {"var": 0, "tm": tm}, {"var": 0, "tm": (tm + 1) % 32}

    def remote(src, dst, send, recv, device):
        return pltpu.make_async_remote_copy(
            src_ref=src, dst_ref=dst, send_sem=send, recv_sem=recv, device_id=device, device_id_type=MESH
        )

    pending = []

    def send(src, dst, ssem, rsem, device, when=None):
        if when is None:
            remote(src, dst, ssem, rsem, device).start()
        else:
            @pl.when(when)
            def _():
                remote(src, dst, ssem, rsem, device).start()

    def sent(src, ssem, when=None):
        pending.append((src, ssem, when))

    def arrived(dst, rsem):
        remote(dst, dst, rsem, rsem, sib).wait_recv()

    barrier = pltpu.get_barrier_semaphore()

    def greet(device):
        pl.semaphore_signal(barrier, inc=1, device_id=device, device_id_type=MESH)

    for device in (x_left, x_right, sib, y_next, y_prev, partner, tm_next, tm_prev, src_next):
        greet(device)
    for k in range(1, NZ):
        greet(at(x, yh, c, (z + k) % NZ, yl))
    for k in range(1, NL):
        greet(at(x, yh, c, z, (yl + k) % NL))

    @pl.when(var != 0)
    def _():
        greet(src_here)

    own = x * 2 + yh
    lats = latent.at[0]
    inputs = (w_query, w_keyval.at[:, pl.ds(0, HD)], w_keyval.at[:, pl.ds(HD, HD)], w_out)

    def full(p, m, cc):
        return wo.at[m, cc] if p == OP else wqkv.at[p, m, cc]

    def x_half(p, m, cc, h):
        return wo.at[m, cc, :, pl.ds(h * 768, 768)] if p == OP else wqkv.at[p, m, cc, pl.ds(h * 48, 48), :]

    def y_blk(p, m, cc, pr, d):
        if p == OP:
            return wo.at[m, cc, :, pl.ds(pl.multiple_of(pr * 768 + d * 384, 128), 384)]
        return wqkv.at[p, m, cc, pl.ds(pl.multiple_of(pr * 48, 16), 48), pl.ds(d * 384, 384)]

    table_in = pltpu.make_async_copy(table, tabv, loc.at[0])
    table_in.start()
    weights_in = [pltpu.make_async_copy(inputs[p], full(p, own, c), loc.at[1 + p]) for p in range(4)]
    for copy in weights_in:
        copy.start()
    latent_in = pltpu.make_async_copy(lats, xw.at[pl.ds(0, CH)], loc.at[5])
    latent_in.start()
    noise_in = pltpu.make_async_copy(noise.at[0], noise_v, loc.at[6])
    noise_in.start()

    ids = prompt_ids[...]
    rows = lax.broadcasted_iota(jnp.int32, (128, PROMPT), 0)
    high = (rows == ids // 128).astype(F32)
    low = (rows == ids % 128).astype(F32)
    counts[...] = lax.dot_general(high, low, (((1,), (1,)), ((), ())), preferred_element_type=F32)
    table_in.wait()

    def add_block(b, acc):
        block = tabv[:, pl.ds(pl.multiple_of(b * 128, 128), 128)].astype(F32)
        return acc + block * counts[pl.ds(b, 1), :]

    total = lax.fori_loop(0, 128, add_block, jnp.zeros((48, 128), F32), unroll=8)
    feature = jnp.sum(total, axis=1, keepdims=True) * (1.0 / PROMPT)
    first = jnp.minimum(48 * tm // 128, 10) * 128
    spot = lax.broadcasted_iota(jnp.int32, (48, 256), 0) + (48 * tm - first)
    lanes = lax.broadcasted_iota(jnp.int32, (48, 256), 1)
    placed = jnp.sum(jnp.where(spot == lanes, feature, 0.0), axis=0, keepdims=True)
    mine[0, :, :] = placed

    @pl.when(var == 0)
    def _():
        mine[1, :, :] = placed

    @pl.when(var != 0)
    def _():
        pl.semaphore_wait(barrier, 18)

    @pl.when(var == 0)
    def _():
        pl.semaphore_wait(barrier, 49)

    @pl.when(var == 0)
    def _():
        for k in range(1, 16):
            remote(mine.at[0], mine.at[1], p0s.at[k], p0r.at[0], {"var": k, "tm": tm}).start()

    for copy in weights_in:
        copy.wait()

    rel = (x, xm, xp, xq)

    def own_sends(p):
        for device, side in ((x_right, 0), (x_left, 1)):
            send(full(p, own, c), full(p, own, c), xs.at[p, side], xr.at[p, side], device)
            sent(full(p, own, c), xs.at[p, side])
        edge_sends(p, 0)
        pair_send(p, 0)

    def edge_sends(p, i):
        m = rel[i] * 2 + yh
        for d, device, edge in ((0, y_next, 3), (1, y_prev, 0)):
            blk = y_blk(p, m, c, par, d)
            send(blk, blk, ys.at[p, i, d], yr.at[p, i, d], device, yl == edge)
            sent(blk, ys.at[p, i, d])

    def pair_send(p, k):
        m = rel[k % 4] * 2 + (yh if k < 4 else 1 - yh)
        send(full(p, m, c), full(p, m, c), ss.at[p, k], sr.at[p, k], sib)
        sent(full(p, m, c), ss.at[p, k])

    def x_first(p):
        for side, i in ((0, 1), (1, 2)):
            m = rel[i] * 2 + yh
            arrived(full(p, m, c), xr.at[p, side])
            half = x_half(p, m, c, side)
            send(half, half, x2s.at[p, side], x2r.at[p, side], (x_right, x_left)[side])
            sent(half, x2s.at[p, side])
            edge_sends(p, i)
            pair_send(p, i)

    def x_second(p):
        m = xq * 2 + yh
        for side in range(2):
            arrived(x_half(p, m, c, side), x2r.at[p, side])
        edge_sends(p, 3)
        pair_send(p, 3)

    def y_step(p, i):
        m = rel[i] * 2 + (1 - yh)
        for d, device, edge in ((0, y_next, 3), (1, y_prev, 0)):
            blk = y_blk(p, m, c, par, d)
            arrived(blk, yr.at[p, i, d])
            send(blk, blk, ys.at[p, i, d], yr.at[p, i, d], device, yl != edge)
            send(blk, blk, zs.at[p, i, d], zr.at[p, i, d], (z_prev, z_next)[d])
            sent(blk, zs.at[p, i, d])

    def z_step(p, i):
        m = rel[i] * 2 + (1 - yh)
        for d in range(2):
            arrived(y_blk(p, m, c, 1 - par, d), zr.at[p, i, d])
        pair_send(p, 4 + i)

    def pair_wait(p):
        for k in range(8):
            m = rel[k % 4] * 2 + (yh if k < 4 else 1 - yh)
            arrived(full(p, m, 1 - c), sr.at[p, k])

    def scatter():
        @pl.when(var == 0)
        def _():
            for k in range(16):
                m, cc = k // 2, k % 2
                cols = pl.ds(cc * HD, HD)
                if k:
                    remote(
                        lats.at[pl.ds(32 * m, 32), cols], sp.at[m, cc, pl.ds(0, 32)], s0s.at[0, k], s0r.at[0], {"var": k, "tm": tm}
                    ).start()
                remote(
                    lats.at[pl.ds(16 * m, 16), cols], sp.at[m, cc, pl.ds(32, 16)], s0s.at[1, k], s0r.at[1], {"var": k, "tm": (tm + 31) % 32}
                ).start()
            pltpu.make_async_copy(lats.at[pl.ds(0, 32), pl.ds(0, HD)], sp.at[0, 0, pl.ds(0, 32)], loc.at[7]).start()

    def source_first():
        @pl.when(var == 0)
        def _():
            pltpu.make_async_copy(lats.at[pl.ds(0, 32), pl.ds(0, HD)], sp.at[0, 0, pl.ds(0, 32)], loc.at[7]).wait()

        @pl.when(var != 0)
        def _():
            arrived(sp.at[own, c, pl.ds(0, 32)], s0r.at[0])

        arrived(sp.at[own, c, pl.ds(32, 16)], s0r.at[1])
        send(sp.at[own, c], sp.at[own, c], s1s.at[0], s1r.at[0], partner)
        sent(sp.at[own, c], s1s.at[0])
        for side, device in ((0, x_right), (1, x_left)):
            send(sp.at[own, c], sp.at[own, c], s2s.at[0, side], s2r.at[0, side], device)
            sent(sp.at[own, c], s2s.at[0, side])

    def source_second():
        m = x * 2 + (1 - yh)
        arrived(sp.at[m, c], s1r.at[0])
        for side, device in ((0, x_right), (1, x_left)):
            send(sp.at[m, c], sp.at[m, c], s2s.at[1, side], s2r.at[1, side], device)
            sent(sp.at[m, c], s2s.at[1, side])

    def source_third():
        for side, i in ((0, 1), (1, 2)):
            m = rel[i] * 2
            for half in range(2):
                hh = yh if half == 0 else 1 - yh
                arrived(sp.at[m + hh, c], s2r.at[half, side])
            blk = sp.at[m + side, c]
            send(blk, blk, s3s.at[side], s3r.at[side], (x_right, x_left)[side])
            sent(blk, s3s.at[side])

    def source_fourth():
        for side in range(2):
            arrived(sp.at[xq * 2 + side, c], s3r.at[side])
        send(sp.at[:, c], sp.at[:, c], s4s.at[0], s4r.at[0], sib)
        sent(sp.at[:, c], s4s.at[0])

    def source_done():
        arrived(sp.at[:, 1 - c], s4r.at[0])

    def pooled_first():
        @pl.when(var != 0)
        def _():
            arrived(mine.at[1], p0r.at[0])

        keep = pltpu.make_async_copy(mine, pooled.at[yl, z], loc.at[8])
        keep.start()
        for k in range(1, NZ):
            send(mine, pooled.at[yl, z], p1s.at[k], p1r.at[k], at(x, yh, c, (z + k) % NZ, yl))
            sent(mine, p1s.at[k])
        keep.wait()

    def pooled_second():
        for k in range(1, NZ):
            arrived(pooled.at[yl, (z + NZ - k) % NZ], p1r.at[k])
        for k in range(1, NL):
            send(pooled.at[yl], pooled.at[yl], p2s.at[k], p2r.at[k], at(x, yh, c, z, (yl + k) % NL))
            sent(pooled.at[yl], p2s.at[k])

    def pooled_third():
        for k in range(1, NL):
            arrived(pooled.at[(yl + NL - k) % NL], p2r.at[k])

    own_sends(QP)
    scatter()
    seam_rows = xw.at[pl.ds(CH, SEAM)]
    send(lats.at[pl.ds(0, SEAM)], seam_rows, seam_s.at[0], seam_r.at[0], tm_prev)
    sent(lats.at[pl.ds(0, SEAM)], seam_s.at[0])
    pooled_first()
    own_sends(KP)
    x_first(QP)
    pooled_second()
    own_sends(VP)
    source_first()
    x_first(KP)
    x_second(QP)
    y_step(QP, 0)
    own_sends(OP)
    source_second()
    for i in range(1, 4):
        y_step(QP, i)
    x_second(KP)
    for i in range(4):
        z_step(QP, i)
    x_first(VP)
    source_third()
    pooled_third()
    for i in range(4):
        y_step(KP, i)
    x_second(VP)
    source_fourth()
    for i in range(4):
        z_step(KP, i)
    x_first(OP)
    for i in range(4):
        y_step(VP, i)
    x_second(OP)
    for i in range(4):
        z_step(VP, i)
    for i in range(4):
        y_step(OP, i)
    for i in range(4):
        z_step(OP, i)
    latent_in.wait()
    arrived(seam_rows, seam_r.at[0])
    source_done()

    cond = embedded[...] + jnp.zeros((1, D), F32)
    pieces_own = [cond[:, 128 * t:128 * (t + 1)] for t in range(12)]
    pieces_src = list(pieces_own)
    for t in range(32):
        first_tile = window_tile(t)
        got = pooled[t % NL, t // NL, 0], pooled[t % NL, t // NL, 1]
        for w in range(2):
            pieces_own[first_tile + w] = pieces_own[first_tile + w] + got[0][:, 128 * w:128 * (w + 1)]
            pieces_src[first_tile + w] = pieces_src[first_tile + w] + got[1][:, 128 * w:128 * (w + 1)]
    gain_own = 1.0 + jnp.concatenate(pieces_own, axis=1)
    gain_src = 1.0 + jnp.concatenate(pieces_src, axis=1)
    for r in range(WIN // 32):
        values = xw[pl.ds(32 * r, 32), :].astype(F32)
        inv = lax.rsqrt(jnp.mean(values * values, axis=-1, keepdims=True) + EPS)
        xn[pl.ds(32 * r, 32), :] = (values * inv * gain_own).astype(BF16)
    for m in range(8):
        values = jnp.concatenate([sp[m, 0], sp[m, 1]], axis=1).astype(F32)
        inv = lax.rsqrt(jnp.mean(values * values, axis=-1, keepdims=True) + EPS)
        rows_out = (values * inv * gain_src).astype(BF16)
        xn[pl.ds(WIN + 32 * m, 32), :] = rows_out[0:32]
        xn[pl.ds(WIN + CH + 16 * m, 16), :] = rows_out[32:48]

    def project(p, t, lo, hi, dst, scale=None):
        w = wqkv[p, :, :, :, pl.ds(256 * t, 256)].reshape(D, 256)
        got = jnp.dot(xn[lo:hi, :], w, preferred_element_type=F32)
        if scale is not None:
            got = got.astype(BF16).astype(F32) * scale
        dst[lo:hi, pl.ds(256 * t, 256)] = got.astype(BF16)

    pair_wait(QP)
    for t in range(3):
        project(QP, t, 0, WIN, q_s, 0.125)
    pair_wait(KP)
    for t in range(3):
        project(KP, t, 0, WIN, k_s)
        project(KP, t, WIN, 2 * WIN, k_s)
    pair_wait(VP)
    for t in range(3):
        project(VP, t, 0, WIN, v_s)
        project(VP, t, WIN, 2 * WIN, v_s)

    beyond = jnp.where(tm == 31, -1e30, 0.0)
    bias = [[(block_table[i, j].astype(F32) - 1.0) * 1e30 for j in range(3)] for i in range(3)]
    for i in range(3):
        bias[i][2] = bias[i][2] + beyond
    lane = lax.broadcasted_iota(jnp.int32, (WIN, 128), 1)
    ramp = (lax.broadcasted_iota(jnp.int32, (SEAM, 128), 0).astype(F32) + 0.5) * (1.0 / SEAM)
    lead_weight = jnp.where(tm == 0, 1.0, ramp)
    ones = jnp.ones((2 * WIN, 128), BF16)

    def head_pair(h, carry):
        cols = pl.ds(pl.multiple_of(h * 128, 128), 128)
        keys = k_s[:, cols]
        values = jnp.concatenate([v_s[:, cols], ones], axis=1)
        queries = q_s[:, cols]
        heads = []
        for e in range(2):
            masked = jnp.where((lane < 64) if e == 0 else (lane >= 64), queries, jnp.zeros_like(queries))
            s_s[e] = lax.dot_general(masked, keys, (((1,), (1,)), ((), ())), preferred_element_type=F32)
        for e in range(2):
            for i in range(3):
                r = pl.ds(128 * i, 128)
                tops = [jnp.maximum(s_s[e, r, pl.ds(128 * j, 128)], s_s[e, r, pl.ds(128 * (j + 3), 128)]) + bias[i][j] for j in range(3)]
                top = jnp.max(jnp.maximum(jnp.maximum(tops[0], tops[1]), tops[2]), axis=-1, keepdims=True)
                for j in range(6):
                    p_s[e, r, pl.ds(128 * j, 128)] = jnp.exp(s_s[e, r, pl.ds(128 * j, 128)] - (top - bias[i][j % 3])).astype(BF16)
            both = jnp.dot(p_s[e], values, preferred_element_type=F32)
            heads.append(both[:, :128] / both[:, 128:])
        attended = jnp.where(lane < 64, heads[0], heads[1])
        tail_out[:, cols] = (attended[CH:] * (1.0 - ramp)).astype(BF16)
        blended[0:SEAM, cols] = attended[0:SEAM] * lead_weight
        blended[SEAM:CH, cols] = attended[SEAM:CH]
        return carry

    lax.fori_loop(0, 6, head_pair, 0)

    send(tail_out, tail_in, tail_s.at[0], tail_r.at[0], tm_next)
    sent(tail_out, tail_s.at[0])
    pair_wait(OP)
    noise_in.wait()
    arrived(tail_in, tail_r.at[0])
    carried = jnp.where(tm == 0, 0.0, tail_in[...].astype(F32))
    mixed = jnp.concatenate([blended[0:SEAM] + carried, blended[SEAM:CH]], axis=0).astype(BF16)
    for t in range(6):
        cols = pl.ds(256 * t, 256)
        w = wo[:, :, :, cols].reshape(HD, 256)
        prediction = jnp.dot(mixed, w, preferred_element_type=F32)
        result = coefs[0] * xw[0:CH, cols].astype(F32) + coefs[1] * prediction + coefs[2] * noise_v[:, cols].astype(F32)
        out[0, :, cols] = result.astype(BF16)

    for src, ssem, _ in pending:
        remote(src, src, ssem, ssem, sib).wait_send()

    @pl.when(var == 0)
    def _():
        for k in range(16):
            if k:
                remote(mine.at[0], mine.at[1], p0s.at[k], p0r.at[0], sib).wait_send()
                blk = sp.at[0, 0, pl.ds(0, 32)]
                remote(blk, blk, s0s.at[0, k], s0r.at[0], sib).wait_send()
            blk = sp.at[0, 0, pl.ds(32, 16)]
            remote(blk, blk, s0s.at[1, k], s0r.at[1], sib).wait_send()


def local(latent, fresh_noise, timestep, prompt_ids, block_table, prompt_table, w_query, w_keyval, w_out):
    current, coef_latent, coef_pred, spread = coefficients(timestep)
    embedded = time_embedding(current)[None, :]
    coefs = jnp.stack([coef_latent, coef_pred, spread])
    anywhere = pl.BlockSpec(memory_space=pl.ANY)
    vmem = pl.BlockSpec(memory_space=pltpu.VMEM)
    smem = pl.BlockSpec(memory_space=pltpu.SMEM)
    dma = pltpu.SemaphoreType.DMA
    return pl.pallas_call(
        kernel,
        out_shape=jax.ShapeDtypeStruct((1, CH, D), BF16),
        in_specs=[anywhere, anywhere, vmem, smem, smem, vmem, anywhere, anywhere, anywhere, anywhere],
        out_specs=vmem,
        scratch_shapes=[
            pltpu.VMEM((3, 8, 2, 96, HD), BF16),
            pltpu.VMEM((8, 2, 48, D), BF16),
            pltpu.VMEM((WIN, D), BF16),
            pltpu.VMEM((8, 2, 48, HD), BF16),
            pltpu.VMEM((2 * WIN, D), BF16),
            pltpu.VMEM((48, 16384), BF16),
            pltpu.VMEM((128, 128), F32),
            pltpu.VMEM((2, 1, 256), F32),
            pltpu.VMEM((NL, NZ, 2, 1, 256), F32),
            pltpu.VMEM((WIN, HD), BF16),
            pltpu.VMEM((2 * WIN, HD), BF16),
            pltpu.VMEM((2 * WIN, HD), BF16),
            pltpu.VMEM((2, WIN, 2 * WIN), F32),
            pltpu.VMEM((2, WIN, 2 * WIN), BF16),
            pltpu.VMEM((CH, HD), F32),
            pltpu.VMEM((SEAM, HD), BF16),
            pltpu.VMEM((SEAM, HD), BF16),
            pltpu.VMEM((CH, D), BF16),
            dma((9,)),
            dma((4, 2)), dma((4, 2)), dma((4, 2)), dma((4, 2)),
            dma((4, 4, 2)), dma((4, 4, 2)), dma((4, 4, 2)), dma((4, 4, 2)),
            dma((4, 8)), dma((4, 8)),
            dma((2, 16)), dma((2,)), dma((1,)), dma((1,)), dma((2, 2)), dma((2, 2)), dma((2,)), dma((2,)), dma((1,)), dma((1,)),
            dma((1,)), dma((1,)), dma((1,)), dma((1,)),
            dma((16,)), dma((1,)), dma((NZ,)), dma((NZ,)), dma((NL,)), dma((NL,)),
        ],
        compiler_params=pltpu.CompilerParams(collective_id=0, has_side_effects=True, vmem_limit_bytes=60 * 1024 * 1024),
    )(latent, fresh_noise, embedded, coefs, block_table, prompt_ids, prompt_table.T, w_query, w_keyval, w_out)


def solution(mesh):
    placed = (
        P("var", "tm", None),
        P("var", "tm", None),
        P(),
        P("var", None),
        P(),
        P(None, "tm"),
        P("var", None),
        P("var", None),
        P("var", None),
    )
    return jax.shard_map(local, mesh=mesh, in_specs=placed, out_specs=P("var", "tm", None), check_vma=False)
```

```python
import math

import jax
import jax.numpy as jnp
from jax import lax
from jax.experimental import pallas as pl
from jax.experimental.pallas import tpu as pltpu
from jax.sharding import PartitionSpec as P

MESH = pl.DeviceIdType.MESH
F32 = jnp.float32
BF16 = jnp.bfloat16

D = 1536
HD = 768
CH = 256
SEAM = 128
WIN = CH + SEAM
PROMPT = 64
TSTEPS = 1000
STRIDE = 200
NX, NZ, NL = 4, 8, 4
LAG = 3
EPS = 1e-06
QP, KP, VP, OP = 0, 1, 2, 3


def plan(moment):
    return jnp.cos((moment / TSTEPS + 0.008) / 1.008 * (math.pi / 2.0)) ** 2


def coefficients(timestep):
    current = timestep[0].astype(F32)
    abar_now = plan(current)
    abar_prev = plan(current - STRIDE)
    spread = jnp.sqrt((1.0 - abar_prev) / (1.0 - abar_now) * (1.0 - abar_now / abar_prev))
    carried = jnp.sqrt((1.0 - abar_prev) * (abar_now / abar_prev - abar_now) / (1.0 - abar_now))
    coef_pred = carried - jnp.sqrt(abar_prev) * jnp.sqrt(1.0 - abar_now) / jnp.sqrt(abar_now)
    coef_latent = jnp.sqrt(abar_prev / abar_now)
    return (current, coef_latent, coef_pred, spread)


def time_embedding(current):
    half_width = D // 2
    frequency = jnp.exp(-math.log(10000.0) * jnp.arange(half_width, dtype=F32) / half_width)
    angles = current * frequency
    return jnp.concatenate([jnp.cos(angles), jnp.sin(angles)])


def window_tile(tm):
    return min(48 * tm // 128, 10)


def kernel(
    latent, noise, embedded, coefs, block_table, prompt_ids, table, w_query, w_keyval, w_out,
    out,
    wts, xw, sp, xn, tabv, counts, mine, pooled, q_s, k_s, v_s, s_s, p_s, blended, tail_out, tail_in, noise_v,
    loc, xs, xr, x2s, x2r, ys, yr, zs, zr, ss, sr,
    s0s, s0r, s1s, s1r, s2s, s2r, s3s, s3r, s4s, s4r, seam_s, seam_r, tail_s, tail_r,
    p0s, p0r, p1s, p1r, p2s, p2r,
):
    var, tm = lax.axis_index("var"), lax.axis_index("tm")
    x, yh, c = var // 4, (var // 2) % 2, var % 2
    z, yl = tm // NL, tm % NL
    par = z % 2
    y = yh * NL + yl
    xm, xp, xq = (x + 3) % NX, (x + 1) % NX, (x + 2) % NX
    y_up, y_dn = (y + 1) % 8, (y + 7) % 8

    def at(x_, yh_, c_, z_, yl_):
        return {"var": (x_ * 2 + yh_) * 2 + c_, "tm": z_ * NL + yl_}

    sib = at(x, yh, 1 - c, z, yl)
    x_left, x_right = at(xm, yh, c, z, yl), at(xp, yh, c, z, yl)
    y_next = at(x, y_up // NL, c, z, y_up % NL)
    y_prev = at(x, y_dn // NL, c, z, y_dn % NL)
    z_next, z_prev = at(x, yh, c, (z + 1) % NZ, yl), at(x, yh, c, (z + 7) % NZ, yl)
    partner = at(x, 1 - yh, c, z, yl)
    tm_next, tm_prev = {"var": var, "tm": (tm + 1) % 32}, {"var": var, "tm": (tm + 31) % 32}
    src_here, src_next = {"var": 0, "tm": tm}, {"var": 0, "tm": (tm + 1) % 32}

    def remote(src, dst, send, recv, device):
        return pltpu.make_async_remote_copy(
            src_ref=src, dst_ref=dst, send_sem=send, recv_sem=recv, device_id=device, device_id_type=MESH
        )

    pending = []

    def send(src, dst, ssem, rsem, device, when=None):
        if when is None:
            remote(src, dst, ssem, rsem, device).start()
        else:
            @pl.when(when)
            def _():
                remote(src, dst, ssem, rsem, device).start()

    def sent(src, ssem, when=None):
        pending.append((src, ssem, when))

    def arrived(dst, rsem):
        remote(dst, dst, rsem, rsem, sib).wait_recv()

    barrier = pltpu.get_barrier_semaphore()

    def greet(device):
        pl.semaphore_signal(barrier, inc=1, device_id=device, device_id_type=MESH)

    for device in (x_left, x_right, sib, y_next, y_prev, partner, tm_next, tm_prev, src_next):
        greet(device)
    for k in range(1, NZ):
        greet(at(x, yh, c, (z + k) % NZ, yl))
    for k in range(1, NL):
        greet(at(x, yh, c, z, (yl + k) % NL))

    @pl.when(var != 0)
    def _():
        greet(src_here)

    own = x * 2 + yh
    lats = latent.at[0]
    inputs = (
        (w_query, (QP, own, c)),
        (w_keyval.at[:, pl.ds(0, HD)], (KP, own, c)),
        (w_keyval.at[:, pl.ds(HD, HD)], (VP, own, c)),
        (w_out.at[:, pl.ds(0, HD)], (OP, own, c, pl.ds(0, 48))),
        (w_out.at[:, pl.ds(HD, HD)], (OP, own, c, pl.ds(48, 48))),
    )

    def full(p, m, cc):
        return wts.at[p, m, cc]

    def x_half(p, m, cc, h):
        return wts.at[p, m, cc, pl.ds(h * 48, 48), :]

    def y_blk(p, m, cc, pr, d):
        return wts.at[p, m, cc, pl.ds(pl.multiple_of(pr * 48, 16), 48), pl.ds(d * 384, 384)]

    table_in = pltpu.make_async_copy(table, tabv, loc.at[0])
    table_in.start()
    weights_in = [pltpu.make_async_copy(src, wts.at[spot_], loc.at[9 + k]) for k, (src, spot_) in enumerate(inputs)]
    for copy in weights_in:
        copy.start()
    latent_in = pltpu.make_async_copy(lats, xw.at[pl.ds(0, CH)], loc.at[5])
    latent_in.start()
    noise_in = pltpu.make_async_copy(noise.at[0], noise_v, loc.at[6])
    noise_in.start()

    ids = prompt_ids[...]
    rows = lax.broadcasted_iota(jnp.int32, (128, PROMPT), 0)
    high = (rows == ids // 128).astype(F32)
    low = (rows == ids % 128).astype(F32)
    counts[...] = lax.dot_general(high, low, (((1,), (1,)), ((), ())), preferred_element_type=F32)
    table_in.wait()

    def add_block(b, acc):
        block = tabv[:, pl.ds(pl.multiple_of(b * 128, 128), 128)].astype(F32)
        return acc + block * counts[pl.ds(b, 1), :]

    total = lax.fori_loop(0, 128, add_block, jnp.zeros((48, 128), F32), unroll=8)
    feature = jnp.sum(total, axis=1, keepdims=True) * (1.0 / PROMPT)
    first = jnp.minimum(48 * tm // 128, 10) * 128
    spot = lax.broadcasted_iota(jnp.int32, (48, 256), 0) + (48 * tm - first)
    lanes = lax.broadcasted_iota(jnp.int32, (48, 256), 1)
    placed = jnp.sum(jnp.where(spot == lanes, feature, 0.0), axis=0, keepdims=True)
    mine[0, :, :] = placed

    @pl.when(var == 0)
    def _():
        mine[1, :, :] = placed

    @pl.when(var != 0)
    def _():
        pl.semaphore_wait(barrier, 18)

    @pl.when(var == 0)
    def _():
        pl.semaphore_wait(barrier, 49)

    @pl.when(var == 0)
    def _():
        for k in range(1, 16):
            remote(mine.at[0], mine.at[1], p0s.at[k], p0r.at[0], {"var": k, "tm": tm}).start()

    for copy in weights_in:
        copy.wait()

    rel = (x, xp, xm, xq)

    def own_sends(p):
        for device, side in ((x_right, 0), (x_left, 1)):
            send(full(p, own, c), full(p, own, c), xs.at[p, side], xr.at[p, side], device)
            sent(full(p, own, c), xs.at[p, side])
        edge_sends(p, 0)
        pair_send(p, 0)

    def edge_sends(p, i):
        m = rel[i] * 2 + yh
        for d, device, edge in ((0, y_next, 3), (1, y_prev, 0)):
            blk = y_blk(p, m, c, par, d)
            send(blk, blk, ys.at[p, i, d], yr.at[p, i, d], device, yl == edge)
            sent(blk, ys.at[p, i, d])

    def pair_send(p, k):
        m = rel[k % 4] * 2 + (yh if k < 4 else 1 - yh)
        send(full(p, m, c), full(p, m, c), ss.at[p, k], sr.at[p, k], sib)
        sent(full(p, m, c), ss.at[p, k])

    def x_first(p):
        for side, i in ((0, 2), (1, 1)):
            m = rel[i] * 2 + yh
            arrived(full(p, m, c), xr.at[p, side])
            half = x_half(p, m, c, side)
            send(half, half, x2s.at[p, side], x2r.at[p, side], (x_right, x_left)[side])
            sent(half, x2s.at[p, side])
            edge_sends(p, i)
            pair_send(p, i)

    def x_second(p):
        m = xq * 2 + yh
        for side in range(2):
            arrived(x_half(p, m, c, side), x2r.at[p, side])
        edge_sends(p, 3)
        pair_send(p, 3)

    def y_item(n, d):
        p, i = n // 4, n % 4
        off = i + i // 2 - 2 * (i // 3)
        m = ((x + off) % NX) * 2 + (1 - yh)
        blk = y_blk(p, m, c, par, d)
        arrived(blk, yr.at[p, i, d])
        send(blk, blk, ys.at[p, i, d], yr.at[p, i, d], (y_next, y_prev)[d], yl != (3, 0)[d])
        send(blk, blk, zs.at[p, i, d], zr.at[p, i, d], (z_prev, z_next)[d])

    def tick(t):
        for d in range(2):
            n = t - LAG * (1 + yl) if d == 0 else t - LAG * (4 - yl)
            if 4 * LAG <= t <= 15 + LAG:
                y_item(n, d)
            elif LAG <= t <= 15 + 4 * LAG:
                @pl.when(jnp.logical_and(n >= 0, n < 16))
                def _():
                    y_item(n, d)
        if t >= 5 * LAG:
            z_step((t - 5 * LAG) // 4, (t - 5 * LAG) % 4)

    def z_step(p, i):
        m = rel[i] * 2 + (1 - yh)
        for d in range(2):
            sent(y_blk(p, m, c, par, d), zs.at[p, i, d])
            arrived(y_blk(p, m, c, 1 - par, d), zr.at[p, i, d])
        pair_send(p, 4 + i)

    def pair_wait(p):
        for k in range(8):
            m = rel[k % 4] * 2 + (yh if k < 4 else 1 - yh)
            arrived(full(p, m, 1 - c), sr.at[p, k])

    def scatter():
        @pl.when(var == 0)
        def _():
            for k in range(16):
                m, cc = k // 2, k % 2
                cols = pl.ds(cc * HD, HD)
                if k:
                    remote(
                        lats.at[pl.ds(32 * m, 32), cols], sp.at[m, cc, pl.ds(0, 32)], s0s.at[0, k], s0r.at[0], {"var": k, "tm": tm}
                    ).start()
                remote(
                    lats.at[pl.ds(16 * m, 16), cols], sp.at[m, cc, pl.ds(32, 16)], s0s.at[1, k], s0r.at[1], {"var": k, "tm": (tm + 31) % 32}
                ).start()
            pltpu.make_async_copy(lats.at[pl.ds(0, 32), pl.ds(0, HD)], sp.at[0, 0, pl.ds(0, 32)], loc.at[7]).start()

    def source_first():
        @pl.when(var == 0)
        def _():
            pltpu.make_async_copy(lats.at[pl.ds(0, 32), pl.ds(0, HD)], sp.at[0, 0, pl.ds(0, 32)], loc.at[7]).wait()

        @pl.when(var != 0)
        def _():
            arrived(sp.at[own, c, pl.ds(0, 32)], s0r.at[0])

        arrived(sp.at[own, c, pl.ds(32, 16)], s0r.at[1])
        send(sp.at[own, c], sp.at[own, c], s1s.at[0], s1r.at[0], partner)
        sent(sp.at[own, c], s1s.at[0])
        for side, device in ((0, x_right), (1, x_left)):
            send(sp.at[own, c], sp.at[own, c], s2s.at[0, side], s2r.at[0, side], device)
            sent(sp.at[own, c], s2s.at[0, side])

    def source_second():
        m = x * 2 + (1 - yh)
        arrived(sp.at[m, c], s1r.at[0])
        for side, device in ((0, x_right), (1, x_left)):
            send(sp.at[m, c], sp.at[m, c], s2s.at[1, side], s2r.at[1, side], device)
            sent(sp.at[m, c], s2s.at[1, side])

    def source_third():
        for side, i in ((0, 2), (1, 1)):
            m = rel[i] * 2
            for half in range(2):
                hh = yh if half == 0 else 1 - yh
                arrived(sp.at[m + hh, c], s2r.at[half, side])
            blk = sp.at[m + side, c]
            send(blk, blk, s3s.at[side], s3r.at[side], (x_right, x_left)[side])
            sent(blk, s3s.at[side])

    def source_fourth():
        for side in range(2):
            arrived(sp.at[xq * 2 + side, c], s3r.at[side])
        send(sp.at[:, c], sp.at[:, c], s4s.at[0], s4r.at[0], sib)
        sent(sp.at[:, c], s4s.at[0])

    def source_done():
        arrived(sp.at[:, 1 - c], s4r.at[0])

    def pooled_first():
        @pl.when(var != 0)
        def _():
            arrived(mine.at[1], p0r.at[0])

        keep = pltpu.make_async_copy(mine, pooled.at[yl, z], loc.at[8])
        keep.start()
        for k in range(1, NZ):
            send(mine, pooled.at[yl, z], p1s.at[k], p1r.at[k], at(x, yh, c, (z + k) % NZ, yl))
            sent(mine, p1s.at[k])
        keep.wait()

    def pooled_second():
        for k in range(1, NZ):
            arrived(pooled.at[yl, (z + NZ - k) % NZ], p1r.at[k])
        for k in range(1, NL):
            send(pooled.at[yl], pooled.at[yl], p2s.at[k], p2r.at[k], at(x, yh, c, z, (yl + k) % NL))
            sent(pooled.at[yl], p2s.at[k])

    def pooled_third():
        for k in range(1, NL):
            arrived(pooled.at[(yl + NL - k) % NL], p2r.at[k])

    seam_rows = xw.at[pl.ds(CH, SEAM)]

    def seam_send():
        send(lats.at[pl.ds(0, SEAM)], seam_rows, seam_s.at[0], seam_r.at[0], tm_prev)
        sent(lats.at[pl.ds(0, SEAM)], seam_s.at[0])

    def gain(which):
        parts = [1.0 + embedded[:, pl.ds(128 * t, 128)] for t in range(12)]
        for t in range(32):
            first_tile = window_tile(t)
            got = pooled[t % NL, t // NL, which]
            for w in range(2):
                parts[first_tile + w] = parts[first_tile + w] + got[:, 128 * w:128 * (w + 1)]
        return jnp.concatenate(parts, axis=1)

    def normalize_own():
        latent_in.wait()
        arrived(seam_rows, seam_r.at[0])
        own_gain = gain(0)
        for r in range(WIN // 32):
            values = xw[pl.ds(32 * r, 32), :].astype(F32)
            inv = lax.rsqrt(jnp.mean(values * values, axis=-1, keepdims=True) + EPS)
            xn[pl.ds(32 * r, 32), :] = (values * inv * own_gain).astype(BF16)

    def normalize_source():
        source_gain = gain(1)
        for m in range(8):
            values = jnp.concatenate([sp[m, 0], sp[m, 1]], axis=1).astype(F32)
            inv = lax.rsqrt(jnp.mean(values * values, axis=-1, keepdims=True) + EPS)
            rows_out = (values * inv * source_gain).astype(BF16)
            xn[pl.ds(WIN + 32 * m, 32), :] = rows_out[0:32]
            xn[pl.ds(WIN + CH + 16 * m, 16), :] = rows_out[32:48]

    def project(p, lo, hi):
        dst = (q_s, k_s, v_s)[p]
        for t in range(3):
            w = wts[p, :, :, :, pl.ds(256 * t, 256)].reshape(D, 256)
            got = jnp.dot(xn[lo:hi, :], w, preferred_element_type=F32).astype(BF16)
            if p == QP:
                got = (got.astype(F32) * 0.125).astype(BF16)
            dst[lo:hi, pl.ds(256 * t, 256)] = got

    beyond = jnp.where(tm == 31, -1e30, 0.0)
    bias = [[(block_table[i, j].astype(F32) - 1.0) * 1e30 for j in range(3)] for i in range(3)]
    for i in range(3):
        bias[i][2] = bias[i][2] + beyond

    def soften(lo, hi):
        def head_pair(h, carry):
            cols = pl.ds(pl.multiple_of(h * 128, 128), 128)
            lane = lax.broadcasted_iota(jnp.int32, (WIN, 128), 1)
            keys = k_s[:, cols]
            queries = q_s[:, cols]
            for e in range(2):
                masked = jnp.where((lane < 64) if e == 0 else (lane >= 64), queries, jnp.zeros_like(queries))
                s_s[e] = lax.dot_general(masked, keys, (((1,), (1,)), ((), ())), preferred_element_type=F32)
            for e in range(2):
                for i in range(3):
                    r = pl.ds(128 * i, 128)
                    tops = [jnp.maximum(s_s[e, r, pl.ds(128 * j, 128)], s_s[e, r, pl.ds(128 * (j + 3), 128)]) + bias[i][j] for j in range(3)]
                    top = jnp.max(jnp.maximum(jnp.maximum(tops[0], tops[1]), tops[2]), axis=-1, keepdims=True)
                    for j in range(6):
                        p_s[h, i, e, :, pl.ds(128 * j, 128)] = jnp.exp(s_s[e, r, pl.ds(128 * j, 128)] - (top - bias[i][j % 3])).astype(BF16)
            return carry

        lax.fori_loop(lo, hi, head_pair, 0)

    def weighted(h, lo, hi):
        cols = pl.ds(pl.multiple_of(h * 128, 128), 128)
        values = jnp.concatenate([v_s[:, cols], jnp.ones((2 * WIN, 128), BF16)], axis=1)
        both = jnp.dot(p_s[h, lo:hi].reshape((hi - lo) * 256, 2 * WIN), values, preferred_element_type=F32)
        both = (both[:, :128] / both[:, 128:]).reshape(hi - lo, 2, 128, 128)
        lane = lax.broadcasted_iota(jnp.int32, (128, 128), 1)
        return cols, [jnp.where(lane < 64, both[i, 0], both[i, 1]) for i in range(hi - lo)]

    ramp = (lax.broadcasted_iota(jnp.int32, (SEAM, 128), 0).astype(F32) + 0.5) * (1.0 / SEAM)
    lead_weight = jnp.where(tm == 0, 1.0, ramp)

    def tails():
        def head_pair(h, carry):
            cols, (last,) = weighted(h, 2, 3)
            tail_out[:, cols] = (last * (1.0 - ramp)).astype(BF16)
            return carry

        lax.fori_loop(0, 6, head_pair, 0)

    def bodies():
        def head_pair(h, carry):
            cols, (lead, rest) = weighted(h, 0, 2)
            blended[0:SEAM, cols] = lead * lead_weight
            blended[SEAM:CH, cols] = rest
            return carry

        lax.fori_loop(0, 6, head_pair, 0)

    last = 16 + 5 * LAG
    steps = {t: [] for t in range(last)}

    def put(t, *step):
        steps[t].append(step)

    for p in range(4):
        put(4 * p + 1, x_first, p)
        put(4 * p + 3, x_second, p)
    put(1, own_sends, VP)
    put(3, own_sends, OP)
    put(6, pooled_second)
    put(12, pooled_third)
    put(14, source_first)
    put(17, source_second)
    put(21, source_third)
    put(25, source_fourth)
    put(18, normalize_own)
    put(21, pair_wait, QP)
    put(21, project, QP, 0, WIN)
    put(25, pair_wait, KP)
    put(25, project, KP, 0, WIN)
    put(28, source_done)
    put(28, normalize_source)
    put(29, project, KP, WIN, 2 * WIN)
    own_sends(QP)
    seam_send()
    own_sends(KP)
    pooled_first()
    scatter()
    for t in range(last):
        for step in steps[t]:
            step[0](*step[1:])
        tick(t)
    soften(0, 6)
    pair_wait(VP)
    project(VP, 0, WIN)
    project(VP, WIN, 2 * WIN)
    tails()
    send(tail_out, tail_in, tail_s.at[0], tail_r.at[0], tm_next)
    sent(tail_out, tail_s.at[0])
    bodies()
    pair_wait(OP)
    noise_in.wait()
    arrived(tail_in, tail_r.at[0])
    carried = jnp.where(tm == 0, 0.0, tail_in[...].astype(F32))
    mixed = jnp.concatenate([blended[0:SEAM] + carried, blended[SEAM:CH]], axis=0).astype(BF16)
    for t in range(6):
        cols = pl.ds(256 * t, 256)
        w = wts[OP, :, :, pl.ds(48 * (t // 3), 48), pl.ds(256 * (t % 3), 256)].reshape(HD, 256)
        prediction = jnp.dot(mixed, w, preferred_element_type=F32)
        result = coefs[0] * xw[0:CH, cols].astype(F32) + coefs[1] * prediction + coefs[2] * noise_v[:, cols].astype(F32)
        out[0, :, cols] = result.astype(BF16)

    for src, ssem, _ in pending:
        remote(src, src, ssem, ssem, sib).wait_send()

    @pl.when(var == 0)
    def _():
        for k in range(16):
            if k:
                remote(mine.at[0], mine.at[1], p0s.at[k], p0r.at[0], sib).wait_send()
                blk = sp.at[0, 0, pl.ds(0, 32)]
                remote(blk, blk, s0s.at[0, k], s0r.at[0], sib).wait_send()
            blk = sp.at[0, 0, pl.ds(32, 16)]
            remote(blk, blk, s0s.at[1, k], s0r.at[1], sib).wait_send()


def local(latent, fresh_noise, timestep, prompt_ids, block_table, prompt_table, w_query, w_keyval, w_out):
    current, coef_latent, coef_pred, spread = coefficients(timestep)
    embedded = time_embedding(current)[None, :]
    coefs = jnp.stack([coef_latent, coef_pred, spread])
    anywhere = pl.BlockSpec(memory_space=pl.ANY)
    vmem = pl.BlockSpec(memory_space=pltpu.VMEM)
    smem = pl.BlockSpec(memory_space=pltpu.SMEM)
    dma = pltpu.SemaphoreType.DMA
    return pl.pallas_call(
        kernel,
        out_shape=jax.ShapeDtypeStruct((1, CH, D), BF16),
        in_specs=[anywhere, anywhere, vmem, smem, smem, vmem, anywhere, anywhere, anywhere, anywhere],
        out_specs=vmem,
        scratch_shapes=[
            pltpu.VMEM((4, 8, 2, 96, HD), BF16),
            pltpu.VMEM((WIN, D), BF16),
            pltpu.VMEM((8, 2, 48, HD), BF16),
            pltpu.VMEM((2 * WIN, D), BF16),
            pltpu.VMEM((48, 16384), BF16),
            pltpu.VMEM((128, 128), F32),
            pltpu.VMEM((2, 1, 256), F32),
            pltpu.VMEM((NL, NZ, 2, 1, 256), F32),
            pltpu.VMEM((WIN, HD), BF16),
            pltpu.VMEM((2 * WIN, HD), BF16),
            pltpu.VMEM((2 * WIN, HD), BF16),
            pltpu.VMEM((2, WIN, 2 * WIN), F32),
            pltpu.VMEM((6, 3, 2, 128, 2 * WIN), BF16),
            pltpu.VMEM((CH, HD), F32),
            pltpu.VMEM((SEAM, HD), BF16),
            pltpu.VMEM((SEAM, HD), BF16),
            pltpu.VMEM((CH, D), BF16),
            dma((14,)),
            dma((4, 2)), dma((4, 2)), dma((4, 2)), dma((4, 2)),
            dma((4, 4, 2)), dma((4, 4, 2)), dma((4, 4, 2)), dma((4, 4, 2)),
            dma((4, 8)), dma((4, 8)),
            dma((2, 16)), dma((2,)), dma((1,)), dma((1,)), dma((2, 2)), dma((2, 2)), dma((2,)), dma((2,)), dma((1,)), dma((1,)),
            dma((1,)), dma((1,)), dma((1,)), dma((1,)),
            dma((16,)), dma((1,)), dma((NZ,)), dma((NZ,)), dma((NL,)), dma((NL,)),
        ],
        compiler_params=pltpu.CompilerParams(collective_id=0, has_side_effects=True, vmem_limit_bytes=60 * 1024 * 1024),
    )(latent, fresh_noise, embedded, coefs, block_table, prompt_ids, prompt_table.T, w_query, w_keyval, w_out)


def solution(mesh):
    placed = (
        P("var", "tm", None),
        P("var", "tm", None),
        P(),
        P("var", None),
        P(),
        P(None, "tm"),
        P("var", None),
        P("var", None),
        P("var", None),
    )
    return jax.shard_map(local, mesh=mesh, in_specs=placed, out_specs=P("var", "tm", None), check_vma=False)
```

```python
import math

import jax
import jax.numpy as jnp
from jax import lax
from jax.experimental import pallas as pl
from jax.experimental.pallas import tpu as pltpu
from jax.sharding import PartitionSpec as P

MESH = pl.DeviceIdType.MESH
F32 = jnp.float32
BF16 = jnp.bfloat16

D = 1536
HD = 768
CH = 256
SEAM = 128
WIN = CH + SEAM
PROMPT = 64
TSTEPS = 1000
STRIDE = 200
NX, NZ, NL = 4, 8, 4
LAG = 3
EPS = 1e-06
QP, KP, VP, OP = 0, 1, 2, 3


def plan(moment):
    return jnp.cos((moment / TSTEPS + 0.008) / 1.008 * (math.pi / 2.0)) ** 2


def coefficients(timestep):
    current = timestep[0].astype(F32)
    abar_now = plan(current)
    abar_prev = plan(current - STRIDE)
    spread = jnp.sqrt((1.0 - abar_prev) / (1.0 - abar_now) * (1.0 - abar_now / abar_prev))
    carried = jnp.sqrt((1.0 - abar_prev) * (abar_now / abar_prev - abar_now) / (1.0 - abar_now))
    coef_pred = carried - jnp.sqrt(abar_prev) * jnp.sqrt(1.0 - abar_now) / jnp.sqrt(abar_now)
    coef_latent = jnp.sqrt(abar_prev / abar_now)
    return (current, coef_latent, coef_pred, spread)


def time_embedding(current):
    half_width = D // 2
    frequency = jnp.exp(-math.log(10000.0) * jnp.arange(half_width, dtype=F32) / half_width)
    angles = current * frequency
    return jnp.concatenate([jnp.cos(angles), jnp.sin(angles)])


def window_tile(tm):
    return min(48 * tm // 128, 10)


def kernel(
    latent, noise, embedded, coefs, block_table, prompt_ids, table, w_query, w_keyval, w_out,
    out,
    wts, xw, sp, xn, tabv, counts, mine, pooled, q_s, k_s, v_s, s_s, p_s, blended, tail_out, tail_in, noise_v,
    loc, xs, xr, x2s, x2r, ys, yr, zs, zr, ss, sr,
    s0s, s0r, s1s, s1r, s2s, s2r, s3s, s3r, s4s, s4r, seam_s, seam_r, tail_s, tail_r,
    p0s, p0r, p1s, p1r, p2s, p2r,
):
    var, tm = lax.axis_index("var"), lax.axis_index("tm")
    x, yh, c = var // 4, (var // 2) % 2, var % 2
    z, yl = tm // NL, tm % NL
    par = z % 2
    y = yh * NL + yl
    xm, xp, xq = (x + 3) % NX, (x + 1) % NX, (x + 2) % NX
    y_up, y_dn = (y + 1) % 8, (y + 7) % 8

    def at(x_, yh_, c_, z_, yl_):
        return {"var": (x_ * 2 + yh_) * 2 + c_, "tm": z_ * NL + yl_}

    sib = at(x, yh, 1 - c, z, yl)
    x_left, x_right = at(xm, yh, c, z, yl), at(xp, yh, c, z, yl)
    y_next = at(x, y_up // NL, c, z, y_up % NL)
    y_prev = at(x, y_dn // NL, c, z, y_dn % NL)
    z_next, z_prev = at(x, yh, c, (z + 1) % NZ, yl), at(x, yh, c, (z + 7) % NZ, yl)
    partner = at(x, 1 - yh, c, z, yl)
    tm_next, tm_prev = {"var": var, "tm": (tm + 1) % 32}, {"var": var, "tm": (tm + 31) % 32}
    src_here, src_next = {"var": 0, "tm": tm}, {"var": 0, "tm": (tm + 1) % 32}

    def remote(src, dst, send, recv, device):
        return pltpu.make_async_remote_copy(
            src_ref=src, dst_ref=dst, send_sem=send, recv_sem=recv, device_id=device, device_id_type=MESH
        )

    pending = []

    def send(src, dst, ssem, rsem, device, when=None):
        if when is None:
            remote(src, dst, ssem, rsem, device).start()
        else:
            @pl.when(when)
            def _():
                remote(src, dst, ssem, rsem, device).start()

    def sent(src, ssem, when=None):
        pending.append((src, ssem, when))

    def arrived(dst, rsem):
        remote(dst, dst, rsem, rsem, sib).wait_recv()

    barrier = pltpu.get_barrier_semaphore()

    def greet(device):
        pl.semaphore_signal(barrier, inc=1, device_id=device, device_id_type=MESH)

    for device in (x_left, x_right, sib, y_next, y_prev, partner, tm_next, tm_prev, src_next):
        greet(device)
    for k in range(1, NZ):
        greet(at(x, yh, c, (z + k) % NZ, yl))
    for k in range(1, NL):
        greet(at(x, yh, c, z, (yl + k) % NL))

    @pl.when(var != 0)
    def _():
        greet(src_here)

    own = x * 2 + yh
    lats = latent.at[0]
    inputs = (
        (w_query, (QP, own, c)),
        (w_keyval.at[:, pl.ds(0, HD)], (KP, own, c)),
        (w_keyval.at[:, pl.ds(HD, HD)], (VP, own, c)),
        (w_out.at[:, pl.ds(0, HD)], (OP, own, c, pl.ds(0, 48))),
        (w_out.at[:, pl.ds(HD, HD)], (OP, own, c, pl.ds(48, 48))),
    )

    def full(p, m, cc):
        return wts.at[p, m, cc]

    def x_half(p, m, cc, h):
        return wts.at[p, m, cc, pl.ds(h * 48, 48), :]

    def y_blk(p, m, cc, pr, d):
        return wts.at[p, m, cc, pl.ds(pl.multiple_of(pr * 48, 16), 48), pl.ds(d * 384, 384)]

    table_in = pltpu.make_async_copy(table, tabv, loc.at[0])
    table_in.start()
    weights_in = [pltpu.make_async_copy(src, wts.at[spot_], loc.at[9 + k]) for k, (src, spot_) in enumerate(inputs)]
    for copy in weights_in:
        copy.start()
    latent_in = pltpu.make_async_copy(lats, xw.at[pl.ds(0, CH)], loc.at[5])
    latent_in.start()
    noise_in = pltpu.make_async_copy(noise.at[0], noise_v, loc.at[6])
    noise_in.start()

    ids = prompt_ids[...]
    rows = lax.broadcasted_iota(jnp.int32, (128, PROMPT), 0)
    high = (rows == ids // 128).astype(F32)
    low = (rows == ids % 128).astype(F32)
    counts[...] = lax.dot_general(high, low, (((1,), (1,)), ((), ())), preferred_element_type=F32)
    table_in.wait()

    def add_block(b, acc):
        block = tabv[:, pl.ds(pl.multiple_of(b * 128, 128), 128)].astype(F32)
        return acc + block * counts[pl.ds(b, 1), :]

    total = lax.fori_loop(0, 128, add_block, jnp.zeros((48, 128), F32), unroll=8)
    feature = jnp.sum(total, axis=1, keepdims=True) * (1.0 / PROMPT)
    first = jnp.minimum(48 * tm // 128, 10) * 128
    spot = lax.broadcasted_iota(jnp.int32, (48, 256), 0) + (48 * tm - first)
    lanes = lax.broadcasted_iota(jnp.int32, (48, 256), 1)
    placed = jnp.sum(jnp.where(spot == lanes, feature, 0.0), axis=0, keepdims=True)
    mine[0, :, :] = placed

    @pl.when(var == 0)
    def _():
        mine[1, :, :] = placed

    @pl.when(var != 0)
    def _():
        pl.semaphore_wait(barrier, 18)

    @pl.when(var == 0)
    def _():
        pl.semaphore_wait(barrier, 49)

    @pl.when(var == 0)
    def _():
        for k in range(1, 16):
            remote(mine.at[0], mine.at[1], p0s.at[k], p0r.at[0], {"var": k, "tm": tm}).start()

    for copy in weights_in:
        copy.wait()

    rel = (x, xp, xm, xq)

    def own_sends(p):
        for device, side in ((x_right, 0), (x_left, 1)):
            send(full(p, own, c), full(p, own, c), xs.at[p, side], xr.at[p, side], device)
            sent(full(p, own, c), xs.at[p, side])
        edge_sends(p, 0)
        pair_send(p, 0)

    def edge_sends(p, i):
        m = rel[i] * 2 + yh
        for d, device, edge in ((0, y_next, 3), (1, y_prev, 0)):
            blk = y_blk(p, m, c, par, d)
            send(blk, blk, ys.at[p, i, d], yr.at[p, i, d], device, yl == edge)
            sent(blk, ys.at[p, i, d])

    def pair_send(p, k):
        m = rel[k % 4] * 2 + (yh if k < 4 else 1 - yh)
        send(full(p, m, c), full(p, m, c), ss.at[p, k], sr.at[p, k], sib)
        sent(full(p, m, c), ss.at[p, k])

    def x_first(p):
        for side, i in ((0, 2), (1, 1)):
            m = rel[i] * 2 + yh
            arrived(full(p, m, c), xr.at[p, side])
            half = x_half(p, m, c, side)
            send(half, half, x2s.at[p, side], x2r.at[p, side], (x_right, x_left)[side])
            sent(half, x2s.at[p, side])
            edge_sends(p, i)
            pair_send(p, i)

    def x_second(p):
        m = xq * 2 + yh
        for side in range(2):
            arrived(x_half(p, m, c, side), x2r.at[p, side])
        edge_sends(p, 3)
        pair_send(p, 3)

    def y_item(n, d):
        p, i = n // 4, n % 4
        off = i + i // 2 - 2 * (i // 3)
        m = ((x + off) % NX) * 2 + (1 - yh)
        blk = y_blk(p, m, c, par, d)
        arrived(blk, yr.at[p, i, d])
        send(blk, blk, ys.at[p, i, d], yr.at[p, i, d], (y_next, y_prev)[d], yl != (3, 0)[d])
        send(blk, blk, zs.at[p, i, d], zr.at[p, i, d], (z_prev, z_next)[d])

    def tick(t):
        for d in range(2):
            n = t - LAG * (1 + yl) if d == 0 else t - LAG * (4 - yl)
            if 4 * LAG <= t <= 15 + LAG:
                y_item(n, d)
            elif LAG <= t <= 15 + 4 * LAG:
                @pl.when(jnp.logical_and(n >= 0, n < 16))
                def _():
                    y_item(n, d)
        if t >= 5 * LAG:
            z_step((t - 5 * LAG) // 4, (t - 5 * LAG) % 4)

    def z_step(p, i):
        m = rel[i] * 2 + (1 - yh)
        for d in range(2):
            sent(y_blk(p, m, c, par, d), zs.at[p, i, d])
            arrived(y_blk(p, m, c, 1 - par, d), zr.at[p, i, d])
        pair_send(p, 4 + i)

    def pair_wait(p):
        for k in range(8):
            m = rel[k % 4] * 2 + (yh if k < 4 else 1 - yh)
            arrived(full(p, m, 1 - c), sr.at[p, k])

    def scatter():
        @pl.when(var == 0)
        def _():
            for k in range(16):
                m, cc = k // 2, k % 2
                cols = pl.ds(cc * HD, HD)
                if k:
                    remote(
                        lats.at[pl.ds(32 * m, 32), cols], sp.at[m, cc, pl.ds(0, 32)], s0s.at[0, k], s0r.at[0], {"var": k, "tm": tm}
                    ).start()
                remote(
                    lats.at[pl.ds(16 * m, 16), cols], sp.at[m, cc, pl.ds(32, 16)], s0s.at[1, k], s0r.at[1], {"var": k, "tm": (tm + 31) % 32}
                ).start()
            pltpu.make_async_copy(lats.at[pl.ds(0, 32), pl.ds(0, HD)], sp.at[0, 0, pl.ds(0, 32)], loc.at[7]).start()

    def source_first():
        @pl.when(var == 0)
        def _():
            pltpu.make_async_copy(lats.at[pl.ds(0, 32), pl.ds(0, HD)], sp.at[0, 0, pl.ds(0, 32)], loc.at[7]).wait()

        @pl.when(var != 0)
        def _():
            arrived(sp.at[own, c, pl.ds(0, 32)], s0r.at[0])

        arrived(sp.at[own, c, pl.ds(32, 16)], s0r.at[1])
        send(sp.at[own, c], sp.at[own, c], s1s.at[0], s1r.at[0], partner)
        sent(sp.at[own, c], s1s.at[0])
        for side, device in ((0, x_right), (1, x_left)):
            send(sp.at[own, c], sp.at[own, c], s2s.at[0, side], s2r.at[0, side], device)
            sent(sp.at[own, c], s2s.at[0, side])

    def source_second():
        m = x * 2 + (1 - yh)
        arrived(sp.at[m, c], s1r.at[0])
        for side, device in ((0, x_right), (1, x_left)):
            send(sp.at[m, c], sp.at[m, c], s2s.at[1, side], s2r.at[1, side], device)
            sent(sp.at[m, c], s2s.at[1, side])

    def source_third():
        for side, i in ((0, 2), (1, 1)):
            m = rel[i] * 2
            for half in range(2):
                hh = yh if half == 0 else 1 - yh
                arrived(sp.at[m + hh, c], s2r.at[half, side])
            blk = sp.at[m + side, c]
            send(blk, blk, s3s.at[side], s3r.at[side], (x_right, x_left)[side])
            sent(blk, s3s.at[side])

    def source_fourth():
        for side in range(2):
            arrived(sp.at[xq * 2 + side, c], s3r.at[side])
        send(sp.at[:, c], sp.at[:, c], s4s.at[0], s4r.at[0], sib)
        sent(sp.at[:, c], s4s.at[0])

    def source_done():
        arrived(sp.at[:, 1 - c], s4r.at[0])

    def pooled_first():
        @pl.when(var != 0)
        def _():
            arrived(mine.at[1], p0r.at[0])

        keep = pltpu.make_async_copy(mine, pooled.at[yl, z], loc.at[8])
        keep.start()
        for k in range(1, NZ):
            send(mine, pooled.at[yl, z], p1s.at[k], p1r.at[k], at(x, yh, c, (z + k) % NZ, yl))
            sent(mine, p1s.at[k])
        keep.wait()

    def pooled_second():
        for k in range(1, NZ):
            arrived(pooled.at[yl, (z + NZ - k) % NZ], p1r.at[k])
        for k in range(1, NL):
            send(pooled.at[yl], pooled.at[yl], p2s.at[k], p2r.at[k], at(x, yh, c, z, (yl + k) % NL))
            sent(pooled.at[yl], p2s.at[k])

    def pooled_third():
        for k in range(1, NL):
            arrived(pooled.at[(yl + NL - k) % NL], p2r.at[k])

    seam_rows = xw.at[pl.ds(CH, SEAM)]

    def seam_send():
        send(lats.at[pl.ds(0, SEAM)], seam_rows, seam_s.at[0], seam_r.at[0], tm_prev)
        sent(lats.at[pl.ds(0, SEAM)], seam_s.at[0])

    def gain(which):
        parts = [1.0 + embedded[:, pl.ds(128 * t, 128)] for t in range(12)]
        for t in range(32):
            first_tile = window_tile(t)
            got = pooled[t % NL, t // NL, which]
            for w in range(2):
                parts[first_tile + w] = parts[first_tile + w] + got[:, 128 * w:128 * (w + 1)]
        return jnp.concatenate(parts, axis=1)

    def normalize_own():
        latent_in.wait()
        arrived(seam_rows, seam_r.at[0])
        own_gain = gain(0)
        for r in range(WIN // 32):
            values = xw[pl.ds(32 * r, 32), :].astype(F32)
            inv = lax.rsqrt(jnp.mean(values * values, axis=-1, keepdims=True) + EPS)
            xn[pl.ds(32 * r, 32), :] = (values * inv * own_gain).astype(BF16)

    def normalize_source():
        source_gain = gain(1)
        for m in range(8):
            values = jnp.concatenate([sp[m, 0], sp[m, 1]], axis=1).astype(F32)
            inv = lax.rsqrt(jnp.mean(values * values, axis=-1, keepdims=True) + EPS)
            rows_out = (values * inv * source_gain).astype(BF16)
            xn[pl.ds(WIN + 32 * m, 32), :] = rows_out[0:32]
            xn[pl.ds(WIN + CH + 16 * m, 16), :] = rows_out[32:48]

    def project(p, lo, hi, tiles=(0, 1, 2)):
        dst = (q_s, k_s, v_s)[p]
        for t in tiles:
            w = wts[p, :, :, :, pl.ds(256 * t, 256)].reshape(D, 256)
            got = jnp.dot(xn[lo:hi, :], w, preferred_element_type=F32).astype(BF16)
            if p == QP:
                got = (got.astype(F32) * 0.125).astype(BF16)
            dst[lo:hi, pl.ds(256 * t, 256)] = got

    beyond = jnp.where(tm == 31, -1e30, 0.0)
    bias = [[(block_table[i, j].astype(F32) - 1.0) * 1e30 for j in range(3)] for i in range(3)]
    for i in range(3):
        bias[i][2] = bias[i][2] + beyond

    def soften(lo, hi):
        count = 128 * (hi - lo)

        def head_pair(h, carry):
            cols = pl.ds(pl.multiple_of(h * 128, 128), 128)
            lane = lax.broadcasted_iota(jnp.int32, (count, 128), 1)
            keys = k_s[:, cols]
            queries = q_s[128 * lo:128 * hi, cols]
            for e in range(2):
                masked = jnp.where((lane < 64) if e == 0 else (lane >= 64), queries, jnp.zeros_like(queries))
                s_s[e, 0:count] = lax.dot_general(masked, keys, (((1,), (1,)), ((), ())), preferred_element_type=F32)
            for e in range(2):
                for i in range(lo, hi):
                    r = pl.ds(128 * (i - lo), 128)
                    tops = [jnp.maximum(s_s[e, r, pl.ds(128 * j, 128)], s_s[e, r, pl.ds(128 * (j + 3), 128)]) + bias[i][j] for j in range(3)]
                    top = jnp.max(jnp.maximum(jnp.maximum(tops[0], tops[1]), tops[2]), axis=-1, keepdims=True)
                    for j in range(6):
                        p_s[h, i, e, :, pl.ds(128 * j, 128)] = jnp.exp(s_s[e, r, pl.ds(128 * j, 128)] - (top - bias[i][j % 3])).astype(BF16)
            return carry

        lax.fori_loop(0, 6, head_pair, 0)

    def weighted(h, lo, hi):
        cols = pl.ds(pl.multiple_of(h * 128, 128), 128)
        values = jnp.concatenate([v_s[:, cols], jnp.ones((2 * WIN, 128), BF16)], axis=1)
        both = jnp.dot(p_s[h, lo:hi].reshape((hi - lo) * 256, 2 * WIN), values, preferred_element_type=F32)
        both = (both[:, :128] / both[:, 128:]).reshape(hi - lo, 2, 128, 128)
        lane = lax.broadcasted_iota(jnp.int32, (128, 128), 1)
        return cols, [jnp.where(lane < 64, both[i, 0], both[i, 1]) for i in range(hi - lo)]

    ramp = (lax.broadcasted_iota(jnp.int32, (SEAM, 128), 0).astype(F32) + 0.5) * (1.0 / SEAM)
    lead_weight = jnp.where(tm == 0, 1.0, ramp)

    def tails():
        def head_pair(h, carry):
            cols, (last,) = weighted(h, 2, 3)
            tail_out[:, cols] = (last * (1.0 - ramp)).astype(BF16)
            return carry

        lax.fori_loop(0, 6, head_pair, 0)

    def bodies():
        def head_pair(h, carry):
            cols, (lead, rest) = weighted(h, 0, 2)
            blended[0:SEAM, cols] = lead * lead_weight
            blended[SEAM:CH, cols] = rest
            return carry

        lax.fori_loop(0, 6, head_pair, 0)

    last = 16 + 5 * LAG
    steps = {t: [] for t in range(last)}

    def put(t, *step):
        steps[t].append(step)

    for p in range(4):
        put(4 * p + 1, x_first, p)
        put(4 * p + 3, x_second, p)
    put(1, own_sends, VP)
    put(3, own_sends, OP)
    put(6, pooled_second)
    put(12, pooled_third)
    put(14, source_first)
    put(17, source_second)
    put(21, source_third)
    put(25, source_fourth)
    put(18, normalize_own)
    put(21, pair_wait, QP)
    for k in range(3):
        put(21 + k, project, QP, 0, WIN, (k,))
    put(25, pair_wait, KP)
    for k in range(3):
        put(25 + k, project, KP, 0, WIN, (k,))
    put(28, source_done)
    put(28, normalize_source)
    for k in range(3):
        put(28 + k, project, KP, WIN, 2 * WIN, (k,))
    own_sends(QP)
    seam_send()
    own_sends(KP)
    pooled_first()
    scatter()
    for t in range(last):
        for step in steps[t]:
            step[0](*step[1:])
        tick(t)
    pair_wait(VP)
    project(VP, 0, WIN)
    project(VP, WIN, 2 * WIN)
    soften(2, 3)
    tails()
    send(tail_out, tail_in, tail_s.at[0], tail_r.at[0], tm_next)
    sent(tail_out, tail_s.at[0])
    soften(0, 2)
    bodies()
    pair_wait(OP)
    noise_in.wait()
    arrived(tail_in, tail_r.at[0])
    carried = jnp.where(tm == 0, 0.0, tail_in[...].astype(F32))
    mixed = jnp.concatenate([blended[0:SEAM] + carried, blended[SEAM:CH]], axis=0).astype(BF16)
    for t in range(6):
        cols = pl.ds(256 * t, 256)
        w = wts[OP, :, :, pl.ds(48 * (t // 3), 48), pl.ds(256 * (t % 3), 256)].reshape(HD, 256)
        prediction = jnp.dot(mixed, w, preferred_element_type=F32)
        result = coefs[0] * xw[0:CH, cols].astype(F32) + coefs[1] * prediction + coefs[2] * noise_v[:, cols].astype(F32)
        out[0, :, cols] = result.astype(BF16)

    for src, ssem, _ in pending:
        remote(src, src, ssem, ssem, sib).wait_send()

    @pl.when(var == 0)
    def _():
        for k in range(16):
            if k:
                remote(mine.at[0], mine.at[1], p0s.at[k], p0r.at[0], sib).wait_send()
                blk = sp.at[0, 0, pl.ds(0, 32)]
                remote(blk, blk, s0s.at[0, k], s0r.at[0], sib).wait_send()
            blk = sp.at[0, 0, pl.ds(32, 16)]
            remote(blk, blk, s0s.at[1, k], s0r.at[1], sib).wait_send()


def local(latent, fresh_noise, timestep, prompt_ids, block_table, prompt_table, w_query, w_keyval, w_out):
    current, coef_latent, coef_pred, spread = coefficients(timestep)
    embedded = time_embedding(current)[None, :]
    coefs = jnp.stack([coef_latent, coef_pred, spread])
    anywhere = pl.BlockSpec(memory_space=pl.ANY)
    vmem = pl.BlockSpec(memory_space=pltpu.VMEM)
    smem = pl.BlockSpec(memory_space=pltpu.SMEM)
    dma = pltpu.SemaphoreType.DMA
    return pl.pallas_call(
        kernel,
        out_shape=jax.ShapeDtypeStruct((1, CH, D), BF16),
        in_specs=[anywhere, anywhere, vmem, smem, smem, vmem, anywhere, anywhere, anywhere, anywhere],
        out_specs=vmem,
        scratch_shapes=[
            pltpu.VMEM((4, 8, 2, 96, HD), BF16),
            pltpu.VMEM((WIN, D), BF16),
            pltpu.VMEM((8, 2, 48, HD), BF16),
            pltpu.VMEM((2 * WIN, D), BF16),
            pltpu.VMEM((48, 16384), BF16),
            pltpu.VMEM((128, 128), F32),
            pltpu.VMEM((2, 1, 256), F32),
            pltpu.VMEM((NL, NZ, 2, 1, 256), F32),
            pltpu.VMEM((WIN, HD), BF16),
            pltpu.VMEM((2 * WIN, HD), BF16),
            pltpu.VMEM((2 * WIN, HD), BF16),
            pltpu.VMEM((2, WIN, 2 * WIN), F32),
            pltpu.VMEM((6, 3, 2, 128, 2 * WIN), BF16),
            pltpu.VMEM((CH, HD), F32),
            pltpu.VMEM((SEAM, HD), BF16),
            pltpu.VMEM((SEAM, HD), BF16),
            pltpu.VMEM((CH, D), BF16),
            dma((14,)),
            dma((4, 2)), dma((4, 2)), dma((4, 2)), dma((4, 2)),
            dma((4, 4, 2)), dma((4, 4, 2)), dma((4, 4, 2)), dma((4, 4, 2)),
            dma((4, 8)), dma((4, 8)),
            dma((2, 16)), dma((2,)), dma((1,)), dma((1,)), dma((2, 2)), dma((2, 2)), dma((2,)), dma((2,)), dma((1,)), dma((1,)),
            dma((1,)), dma((1,)), dma((1,)), dma((1,)),
            dma((16,)), dma((1,)), dma((NZ,)), dma((NZ,)), dma((NL,)), dma((NL,)),
        ],
        compiler_params=pltpu.CompilerParams(collective_id=0, has_side_effects=True, vmem_limit_bytes=60 * 1024 * 1024),
    )(latent, fresh_noise, embedded, coefs, block_table, prompt_ids, prompt_table.T, w_query, w_keyval, w_out)


def solution(mesh):
    placed = (
        P("var", "tm", None),
        P("var", "tm", None),
        P(),
        P("var", None),
        P(),
        P(None, "tm"),
        P("var", None),
        P("var", None),
        P("var", None),
    )
    return jax.shard_map(local, mesh=mesh, in_specs=placed, out_specs=P("var", "tm", None), check_vma=False)
```
